32 devices in a mesh: cuts: 4 (over x, core), dom: 4 (over z), vec: 2 (over y).
Axes of the slice: x: 2, y: 2, z: 4, core: 2. Of those that a mesh axis runs over, the one named last changes fastest.
Arguments:
- starts_old: bfloat16 [4, 2, 32, 384, 768], P('cuts', None, 'vec', 'dom'), may hold values from -6 to 6
- y_operator: bfloat16 [768, 768], replicated, may hold values from -0.21875 to 0.21875
- coarse_inverse: bfloat16 [384, 384], P('vec'), may hold values from -1 to 2
- base_speed: float32 [384, 768], P('dom'), may hold values from 0.5 to 1.5
- damping: float32 [32], P('vec'), may hold values from 0.5 to 3
- coupling: float32 [32], P('vec'), may hold values from 0.3 to 1.5
Outputs:
- ends_new: float32 [4, 2, 32, 384, 768], P('cuts', None, 'vec', 'dom')
The draws below stay inside these ranges and needn't reach their ends.
All inputs are finite; a program needn't handle non-finite values.
Results may differ from the reference program's by a relative error of at most 0.0078.
Values may be sent and summed in bfloat16 or wider, within the bound.
No kernel may reach another device: no remote copies, remote signals or barrier semaphores. Data moves between devices by JAX's collectives and lax.ppermute only.
A program may use at most 192 MiB of HBM per device.

```python
import math
import jax
import jax.numpy as jnp
import numpy as np
from jax import lax

WAVES = 32
NY = 768
NP = 16
NX = 384
SLICES = 4


def draw_coarse_inverse(key, part):
    noise = jax.random.normal(key, (NX, NX), jnp.float32)
    matrix = jnp.eye(NX, dtype=jnp.float32) + 0.3 * noise / math.sqrt(NX)
    return matrix.astype(jnp.bfloat16)


def steps_of(stream_key, shape, shards, least, top_value):
    gain, own = 1.0, jax.random.fold_in(stream_key, 6)
    for axis_at, blocks in shards:
        steps = jnp.exp(jax.random.uniform(jax.random.fold_in(own, axis_at), (blocks,), jnp.float32, least / len(shards), top_value / len(shards)))
        gain = gain * jnp.repeat(steps, shape[axis_at] // blocks).reshape([-1 if axis == axis_at else 1 for axis in range(len(shape))])
    return gain


def bell_draw(own_key, extent, deviation, reach, pieces=(), held_as=jnp.bfloat16):
    gain = steps_of(own_key, extent, pieces, -0.22, 0.18) if pieces else 1.0
    drawn = jax.random.normal(own_key, extent, jnp.float32) * deviation * gain
    return jnp.minimum(jnp.maximum(drawn, -reach), reach).astype(held_as)


def setup_inputs(seed: int = 0) -> dict:
    keys = jax.random.split(jax.random.key(seed), 7)
    starts_old = bell_draw(keys[0], (SLICES, 2, WAVES, NX, NY), 1.0, 6.0, ((0, 4), (2, 2), (3, 4)))
    y_operator = bell_draw(keys[1], (NY, NY), NY ** -0.5, 0.21875)
    coarse_inverse = draw_coarse_inverse(jax.random.fold_in(keys[6], 71), 0)
    base_speed = jnp.clip(0.5 + 1.0 * jax.random.uniform(keys[3], (NX, NY), jnp.float32) ** steps_of(keys[3], (NX, NY), ((0, 4),), -0.2, 0.2), 0.5, 1.5)
    damping = jnp.clip(jnp.exp(math.log(3.0) - 1.7917595 * jax.random.uniform(keys[4], (WAVES,), jnp.float32) ** steps_of(keys[4], (WAVES,), ((0, 2),), -0.2, 0.2)), 0.5, 3.0)
    coupling = jnp.clip(jnp.exp(math.log(1.5) - 1.60943787 * jax.random.uniform(keys[5], (WAVES,), jnp.float32) ** steps_of(keys[5], (WAVES,), ((0, 2),), -0.2, 0.2)), 0.3, 1.5)
    return {"starts_old": starts_old, "y_operator": y_operator, "coarse_inverse": coarse_inverse, "base_speed": base_speed, "damping": damping, "coupling": coupling}


fine_step = 0.25
penalty = 2.0


def cheb_matrix(points_sub):
    indices = np.arange(points_sub)
    points = -np.cos(np.pi * indices / (points_sub - 1))
    edge_weight = np.where((indices == 0) | (indices == points_sub - 1), 2.0, 1.0)
    sign_table = np.where((indices[:, None] + indices[None, :]) % 2 == 0, 1.0, -1.0)
    identity_table = np.eye(points_sub)
    gap_matrix = points[:, None] - points[None, :] + identity_table
    off_diag = edge_weight[:, None] / edge_weight[None, :] * sign_table / gap_matrix * (1.0 - identity_table)
    return off_diag - off_diag.sum(axis=1)[:, None] * identity_table


def slope_of(values, y_operator, base_speed, damping, coupling, derivative):
    parts, wave_count, column_count, y_count = values.shape
    points_sub = derivative.shape[0]
    x_scale = 4.0 / (points_sub * points_sub)
    rounded = lax.optimization_barrier(values.astype(jnp.bfloat16)).astype(values.dtype)
    along_y = jnp.einsum("pwxk,kj->pwxj", rounded, y_operator.astype(values.dtype), precision=lax.Precision.HIGHEST)
    blocks = values.reshape(parts, wave_count, column_count // points_sub, points_sub, y_count)
    along_x = jnp.einsum("ij,pwsjy->pwsiy", derivative, blocks, precision=lax.Precision.HIGHEST).reshape(values.shape)
    previous = jnp.concatenate([jnp.zeros_like(values[:, :, :1]), values[:, :, :-1]], axis=2)
    first_point = (jnp.arange(column_count) % points_sub == 0).astype(values.dtype)[None, None, :, None]
    jump_term = first_point * (values - previous)
    advect = base_speed[None, None] * (x_scale * along_x + penalty * jump_term)
    sign_factor = jnp.array([1.0, -1.0], values.dtype)[:, None, None, None]
    partner = rounded[::-1]
    return -advect + along_y + sign_factor * coupling[None, :, None, None] * partner - damping[None, :, None, None] * values


def reference(starts_old, y_operator, coarse_inverse, base_speed, damping, coupling):
    derivative = jnp.asarray(cheb_matrix(NP), jnp.float32)
    factor = 1.0 / (1.0 + 2.0 * fine_step * damping)
    inverse_wide = coarse_inverse.astype(jnp.float32)
    ends = []
    last_end = None
    for slice_k in range(SLICES):
        start_now = starts_old[slice_k].astype(jnp.float32)
        middle = start_now + fine_step * slope_of(start_now, y_operator, base_speed, damping, coupling, derivative)
        fine_end = middle + fine_step * slope_of(middle, y_operator, base_speed, damping, coupling, derivative)
        if slice_k == 0:
            end_now = fine_end
        else:
            sent = lax.optimization_barrier(last_end.astype(jnp.bfloat16)).astype(jnp.float32)
            gap = lax.optimization_barrier((sent - start_now).astype(jnp.bfloat16)).astype(jnp.float32)
            mapped = jnp.einsum("ij,pwjy->pwiy", inverse_wide, gap, precision=lax.Precision.HIGHEST)
            end_now = fine_end + factor[None, :, None, None] * mapped
        ends.append(end_now)
        last_end = end_now
    return jnp.stack(ends)
```

```python
import functools

import jax
import jax.numpy as jnp
import numpy as np
from jax import lax
from jax.experimental import pallas as pl
from jax.experimental.pallas import tpu as pltpu
from jax.sharding import PartitionSpec as P

NP = 16
STEP = 0.25
PENALTY = 2.0
BF = jnp.bfloat16
F32 = jnp.float32


def cheb_matrix(points_sub):
    indices = np.arange(points_sub)
    points = -np.cos(np.pi * indices / (points_sub - 1))
    edge_weight = np.where((indices == 0) | (indices == points_sub - 1), 2.0, 1.0)
    sign_table = np.where((indices[:, None] + indices[None, :]) % 2 == 0, 1.0, -1.0)
    identity_table = np.eye(points_sub)
    gap_matrix = points[:, None] - points[None, :] + identity_table
    off_diag = (
        edge_weight[:, None]
        / edge_weight[None, :]
        * sign_table
        / gap_matrix
        * (1.0 - identity_table)
    )
    return off_diag - off_diag.sum(axis=1)[:, None] * identity_table


def advection_matrix(columns):
    subs = columns // NP
    table = np.kron(np.eye(subs), cheb_matrix(NP) * (4.0 / (NP * NP)))
    for first in range(0, columns, NP):
        table[first, first] += PENALTY
        if first:
            table[first, first - 1] -= PENALTY
    return table


def high_low(table):
    table = np.asarray(table, np.float32)
    high = table.astype(BF)
    low = (table - high.astype(np.float32)).astype(BF)
    return np.concatenate([high, low], axis=0)


def smem():
    return pl.BlockSpec(memory_space=pltpu.SMEM)


def whole(shape):
    zeros = (0,) * len(shape)
    return pl.BlockSpec(shape, lambda *_: zeros)


def call(kernel, grid, in_specs, out_specs, out_shape, args, scratch=(), aliases={}, cost=None):
    flops, moved = cost
    return pl.pallas_call(
        kernel,
        grid_spec=pltpu.PrefetchScalarGridSpec(
            num_scalar_prefetch=1,
            grid=grid,
            in_specs=in_specs,
            out_specs=out_specs,
            scratch_shapes=list(scratch),
        ),
        out_shape=out_shape,
        input_output_aliases=aliases,
        cost_estimate=pl.CostEstimate(flops=flops, bytes_accessed=moved, transcendentals=0),
    )(*args)


def edge_kernel(idx, s_ref, y_ref, d_ref, speed_ref, damp_ref, coup_ref, out_ref):
    parts, waves, _, y_count = s_ref.shape
    last = s_ref[:, :, NP - 1, :]
    along_y = jnp.dot(
        last.reshape(parts * waves, y_count), y_ref[...], preferred_element_type=F32
    ).reshape(parts, waves, y_count)
    speed = speed_ref[7:8, :]
    damp = damp_ref[...]
    coup = coup_ref[...]
    for p in range(parts):
        mine = last[p].astype(F32)
        other = last[1 - p].astype(F32)
        along_x = jnp.sum(s_ref[p].astype(F32) * d_ref[...][None], axis=1)
        sign = 1.0 if p == 0 else -1.0
        slope = -speed * along_x + along_y[p] + sign * coup * other - damp * mine
        out_ref[0, p] = mine
        out_ref[1, p] = mine + STEP * slope


def fine_kernel(
    base, ysplit, idx, s_ref, next_ref, halo_ref, y_ref, a_ref, speed_ref, damp_ref, coup_ref,
    f_ref, *rest,
):
    q_refs, (mid_ref, midb_ref, h_ref) = rest[:-3], rest[-3:]
    parts, waves, columns, y_count = s_ref.shape
    rows = parts * waves * columns
    width = 256 if y_count % 256 == 0 else 128
    wave0 = base + pl.program_id(0) * waves
    first = lax.broadcasted_iota(jnp.int32, (8, 1), 0) == 0

    def step(b_ref, wide, kind, lo, store):
        cols = slice(lo, lo + width)
        along_y = jnp.dot(
            b_ref[...].reshape(rows, y_count), y_ref[:, cols], preferred_element_type=F32
        ).reshape(parts, waves, columns, width)
        speed = speed_ref[:, cols]
        for t in range(waves):
            damp = damp_ref[wave0 + t]
            coup = coup_ref[wave0 + t]
            for p in range(parts):
                two = jnp.dot(a_ref[...], b_ref[p, t, :, cols], preferred_element_type=F32)
                along_x = two[:columns] + two[columns:]
                behind = PENALTY * halo_ref[kind, p, t, :, cols]
                top = along_x[:8] - jnp.where(first, behind, 0.0)
                along_x = jnp.concatenate([top, along_x[8:]], axis=0)
                value = wide(p, t, cols)
                partner = b_ref[1 - p, t, :, cols].astype(F32)
                signed = coup if p == 0 else -coup
                slope = along_y[p, t] - speed * along_x + signed * partner - damp * value
                store(p, t, cols, value + STEP * slope)

    def store_mid(p, t, cols, value):
        mid_ref[p, t, :, cols] = value
        midb_ref[p, t, :, cols] = value.astype(BF)

    def store_end(p, t, cols, value):
        f_ref[p, t, :, cols] = value
        h_ref[p, t, :, cols] = (value - next_ref[p, t, :, cols].astype(F32)).astype(BF)

    for lo in range(0, y_count, width):
        step(s_ref, lambda p, t, cols: s_ref[p, t, :, cols].astype(F32), 0, lo, store_mid)
    for lo in range(0, y_count, width):
        step(midb_ref, lambda p, t, cols: mid_ref[p, t, :, cols], 1, lo, store_end)

    quarter = y_count // ysplit
    for a, q_ref in enumerate(q_refs):
        to = idx[0] ^ a
        part = to // ysplit
        lo = pl.multiple_of((to % ysplit) * quarter, 128)
        for t in range(waves):
            q_ref[t] = h_ref[part, t, :, pl.ds(lo, quarter)]


def gather_kernel(cuts, doms, group, idx, *refs):
    r_refs, z_refs = refs[:cuts], refs[cuts:]
    for a, r_ref in enumerate(r_refs):
        source = idx[0] ^ a

        @pl.when(source < cuts - 1)
        def _():
            for b, z_ref in enumerate(z_refs):
                to = idx[1] ^ b
                for t in range(group):
                    z_ref[source, t] = r_ref[to * group + t]


def chain_kernel(base, doms, group, cuts, idx, gain_ref, c_ref, *refs):
    z_refs, t_refs, (line_ref, back_ref) = refs[:doms], refs[doms : 2 * doms], refs[2 * doms :]
    columns = z_refs[0].shape[2]
    total = columns * doms
    block = 384 if total % 384 == 0 else columns
    for t in range(group):
        gain = gain_ref[base + idx[1] * group + t]
        for k in range(cuts - 1):
            for b in range(doms):
                at = pl.ds(pl.multiple_of((idx[1] ^ b) * columns, 16), columns)
                piece = z_refs[b][k, t]
                if k:
                    piece = (piece.astype(F32) + gain * back_ref[at, :]).astype(BF)
                line_ref[at, :] = piece

            def rows(i, _):
                at = pl.ds(pl.multiple_of(i * block, 16), block)
                back_ref[at, :] = jnp.dot(
                    c_ref[at, :], line_ref[...], preferred_element_type=F32
                )
                return _

            if total == block:
                rows(0, 0)
            else:
                lax.fori_loop(0, total // block, rows, 0)
            for b in range(doms):
                at = pl.ds(pl.multiple_of((idx[1] ^ b) * columns, 16), columns)
                t_refs[b][k, t] = back_ref[at, :].astype(BF)


def scatter_kernel(cuts, doms, group, idx, *refs):
    z_refs, u_refs = refs[:doms], refs[doms:]
    for a, u_ref in enumerate(u_refs):
        slot = jnp.maximum((idx[0] ^ a) - 1, 0)
        for b, z_ref in enumerate(z_refs):
            source = idx[1] ^ b
            for t in range(group):
                u_ref[source * group + t] = z_ref[slot, t]


def final_kernel(base, ysplit, cuts, has_out, idx, gain_ref, f_ref, *refs):
    v_refs = refs[:cuts]
    out_ref = refs[-1]
    waves = f_ref.shape[1]
    quarter = f_ref.shape[3] // ysplit
    wave0 = base + pl.program_id(0) * waves
    leader = idx[0] == 0

    @pl.when(leader)
    def _():
        out_ref[0] = f_ref[...]

    @pl.when(jnp.logical_not(leader))
    def _():
        for a, v_ref in enumerate(v_refs):
            source = idx[0] ^ a
            part = source // ysplit
            cols = pl.ds(pl.multiple_of((source % ysplit) * quarter, 128), quarter)
            for t in range(waves):
                gain = gain_ref[wave0 + t]
                out_ref[0, part, t, :, cols] = (
                    f_ref[part, t, :, cols] + gain * v_ref[t].astype(F32)
                )


def local(starts_old, y_operator, coarse_inverse, base_speed, damping, coupling):
    cuts, doms, vecs = (lax.axis_size(name) for name in ("cuts", "dom", "vec"))
    cut, dom, vec = (lax.axis_index(name) for name in ("cuts", "dom", "vec"))
    idx = jnp.stack([cut, dom]).astype(jnp.int32)
    start = starts_old[0]
    parts, waves, columns, y_count = start.shape
    ysplit = cuts // parts
    quarter = y_count // ysplit
    groups = waves // doms
    sizes = [1, groups - 2, 1] if groups > 2 else [1] * groups
    gain = 1.0 / (1.0 + 2.0 * STEP * damping)

    inverse_parts = [coarse_inverse] + [
        lax.ppermute(coarse_inverse, "vec", [(v, v ^ a) for v in range(vecs)])
        for a in range(1, vecs)
    ]
    stacked = jnp.stack(inverse_parts)
    inverse = jnp.concatenate([stacked[vec ^ v] for v in range(vecs)], axis=0)

    last_row = cheb_matrix(NP)[NP - 1] * (4.0 / (NP * NP))
    edges = call(
        edge_kernel,
        (1,),
        [
            pl.BlockSpec((parts, waves, NP, y_count), lambda i, _: (0, 0, columns // NP - 1, 0)),
            whole(y_operator.shape),
            whole((NP, 1)),
            pl.BlockSpec((8, y_count), lambda i, _: (columns // 8 - 1, 0)),
            whole((waves, 1)),
            whole((waves, 1)),
        ],
        whole((2, parts, waves, y_count)),
        jax.ShapeDtypeStruct((2, parts, waves, y_count), F32),
        (
            idx,
            start,
            y_operator,
            jnp.asarray(last_row[:, None], F32),
            base_speed,
            damping[:, None],
            coupling[:, None],
        ),
        cost=(2 * parts * waves * y_count * y_count, 2 * y_count * y_count),
    )
    halo = lax.ppermute(edges, "dom", [(d, d + 1) for d in range(doms - 1)])
    halo = halo.reshape(2, parts, waves, 1, y_count)

    table = jnp.asarray(high_low(advection_matrix(columns)))
    pieces = []
    base = 0
    for group in sizes:
        count = group * doms
        upcoming = lax.ppermute(
            start[:, base : base + count], "cuts", [(k, k - 1) for k in range(1, cuts)]
        )
        pieces.append((base, group, count, upcoming))
        base += count

    state = []
    for base, group, count, upcoming in pieces:
        step = 4 if count % 4 == 0 and base % 4 == 0 else 1
        block = (parts, step, columns, y_count)
        size = parts * count * columns * y_count
        out = call(
            functools.partial(fine_kernel, base, ysplit),
            (count // step,),
            [
                pl.BlockSpec(block, lambda i, _, o=base // step: (0, o + i, 0, 0)),
                pl.BlockSpec(block, lambda i, _: (0, i, 0, 0)),
                pl.BlockSpec(
                    (2, parts, step, 1, y_count), lambda i, _, o=base // step: (0, 0, o + i, 0, 0)
                ),
                whole(y_operator.shape),
                whole(table.shape),
                whole(base_speed.shape),
                smem(),
                smem(),
            ],
            [pl.BlockSpec(block, lambda i, _: (0, i, 0, 0))]
            + [pl.BlockSpec((step, columns, quarter), lambda i, _: (i, 0, 0))] * cuts,
            [jax.ShapeDtypeStruct((parts, count, columns, y_count), F32)]
            + [jax.ShapeDtypeStruct((count, columns, quarter), BF)] * cuts,
            (idx, start, upcoming, halo, y_operator, table, base_speed, damping, coupling),
            scratch=[pltpu.VMEM(block, F32), pltpu.VMEM(block, BF), pltpu.VMEM(block, BF)],
            cost=(4 * size * y_count, 10 * size),
        )
        fine, quarters = out[0], out[1:]
        arrived = [quarters[0]] + [
            lax.ppermute(quarters[a], "cuts", [(k, k ^ a) for k in range(cuts - 1)])
            for a in range(1, cuts)
        ]
        piece = (cuts - 1, group, columns, quarter)
        moved = 4 * cuts * count * columns * quarter
        piece_type = [jax.ShapeDtypeStruct(piece, BF)] * doms
        sorted_pieces = call(
            functools.partial(gather_kernel, cuts, doms, group),
            (1,),
            [whole((count, columns, quarter))] * cuts,
            [whole(piece)] * doms,
            piece_type,
            (idx, *arrived),
            cost=(0, moved),
        )
        lines = [sorted_pieces[0]] + [
            lax.ppermute(sorted_pieces[b], "dom", [(d, d ^ b) for d in range(doms)])
            for b in range(1, doms)
        ]
        total = columns * doms
        corrected = call(
            functools.partial(chain_kernel, base, doms, group, cuts),
            (1,),
            [smem(), whole(inverse.shape)] + [whole(piece)] * doms,
            [whole(piece)] * doms,
            piece_type,
            (idx, gain, inverse, *lines),
            scratch=[pltpu.VMEM((total, quarter), BF), pltpu.VMEM((total, quarter), F32)],
            cost=(2 * (cuts - 1) * group * total * total * quarter, moved),
        )
        back = [corrected[0]] + [
            lax.ppermute(corrected[b], "dom", [(d, d ^ b) for d in range(doms)])
            for b in range(1, doms)
        ]
        by_cut = call(
            functools.partial(scatter_kernel, cuts, doms, group),
            (1,),
            [whole(piece)] * doms,
            [whole((count, columns, quarter))] * cuts,
            [jax.ShapeDtypeStruct((count, columns, quarter), BF)] * cuts,
            (idx, *back),
            cost=(0, moved),
        )
        corrections = [by_cut[0]] + [
            lax.ppermute(by_cut[a], "cuts", [(c, c ^ a) for c in range(cuts) if c ^ a])
            for a in range(1, cuts)
        ]
        state.append((base, count, fine, corrections))

    result = None
    for base, count, fine, corrections in state:
        step = 2 if count % 2 == 0 and base % 2 == 0 else 1
        block = (parts, step, columns, y_count)
        extra = [] if result is None else [result]
        result = call(
            functools.partial(final_kernel, base, ysplit, cuts, result is not None),
            (count // step,),
            [smem(), pl.BlockSpec(block, lambda i, _: (0, i, 0, 0))]
            + [pl.BlockSpec((step, columns, quarter), lambda i, _: (i, 0, 0))] * cuts
            + [pl.BlockSpec(memory_space=pl.ANY)] * len(extra),
            pl.BlockSpec((1, *block), lambda i, _, o=base // step: (0, 0, o + i, 0, 0)),
            jax.ShapeDtypeStruct((1, parts, waves, columns, y_count), F32),
            (idx, gain, fine, *corrections, *extra),
            aliases={3 + cuts: 0} if extra else {},
            cost=(0, 10 * parts * count * columns * y_count),
        )
    return result


def solution(mesh):
    in_specs = (
        P("cuts", None, "vec", "dom", None),
        P(),
        P("vec", None),
        P("dom", None),
        P("vec"),
        P("vec"),
    )
    out_specs = P("cuts", None, "vec", "dom", None)
    return jax.shard_map(local, mesh=mesh, in_specs=in_specs, out_specs=out_specs, check_vma=False)
```
